256 devices in a mesh: views: 8 (over y, core), rows: 16 (over x, z_hi), chan: 2 (over z_lo).
Axes of the slice: x: 4, y: 4, z: 8 (z_hi: 4, z_lo: 2; z = z_hi * 2 + z_lo), core: 2. Of those that a mesh axis runs over, the one named last changes fastest.
Arguments:
- latent: bfloat16 [256, 384, 256], P(('views', 'rows'), 'chan'), parts along dimension 0, may hold values from -6 to 6
- cache_low_a: bfloat16 [2, 256, 384, 256], P(None, ('views', 'rows'), 'chan'), parts along dimension 1, may hold values from -6 to 6
- cache_low_b: bfloat16 [2, 256, 384, 256], P(None, ('views', 'rows'), 'chan'), parts along dimension 1, may hold values from -6 to 6
- gain_low_a: bfloat16 [384], P('chan'), may hold values from 0.5 to 1.5
- gain_low_b: bfloat16 [384], P('chan'), may hold values from 0.5 to 1.5
- kernel_low_a: bfloat16 [3, 3, 3, 384, 384], P(None, None, None, 'chan'), may hold values from -0.0625 to 0.0625
- kernel_low_b: bfloat16 [3, 3, 3, 384, 384], P(None, None, None, 'chan'), may hold values from -0.0625 to 0.0625
- resample_kernel: bfloat16 [3, 3, 192, 384], P(None, None, 'rows'), may hold values from -0.109375 to 0.109375
- gain_high_a: bfloat16 [192], replicated, may hold values from 0.5 to 1.5
- gain_high_b: bfloat16 [192], replicated, may hold values from 0.5 to 1.5
- kernel_high_a: bfloat16 [3, 3, 3, 192, 192], P(None, None, None, 'rows'), may hold values from -0.078125 to 0.078125
- kernel_high_b: bfloat16 [3, 3, 3, 192, 192], P(None, None, None, 'rows'), may hold values from -0.078125 to 0.078125
- cache_high_a: bfloat16 [2, 512, 192, 512], P(None, ('views', 'rows'), None, 'chan'), parts along dimension 1, may hold values from -6 to 6
- cache_high_b: bfloat16 [2, 512, 192, 512], P(None, ('views', 'rows'), None, 'chan'), parts along dimension 1, may hold values from -6 to 6
Outputs:
- decoded: bfloat16 [512, 192, 512], P(('views', 'rows'), None, 'chan'), parts along dimension 0
The draws below stay inside these ranges and needn't reach their ends.
There are 8 independent parts, one for each index of `views`. The reference program is written for one: setup_inputs(seed, part) draws one part's arguments, and reference() takes and returns one part's arrays. A program takes and returns all parts, laid end to end along the dimension named above; an argument that names none is the same for every part. Nothing has to cross between parts.
All inputs are finite; a program needn't handle non-finite values.
Results may differ from the reference program's by a relative error of at most 0.0095.
Values may be sent and summed in bfloat16 or wider, within the bound.
A program may use at most 128 MiB of HBM per device.

```python
import jax
import jax.numpy as jnp
from jax import lax

C1 = 384
C2 = 192
W1 = 256
H1 = 32
H2 = 64
W2 = 512


def block_levels(stream_key, dims, split, low, top_value):
    def one(dim, blocks):
        steps = jax.random.uniform(jax.random.fold_in(jax.random.fold_in(stream_key, 6), dim), (blocks,), jnp.float32, low / len(split), top_value / len(split))
        return jnp.repeat(jnp.exp(steps), dims[dim] // blocks).reshape((-1,) + (1,) * (len(dims) - dim - 1))

    factor_of = one(*split[0])
    for cut in split[1:]:
        factor_of = factor_of * one(*cut)
    return factor_of


def scatter_about(rng, extent, spread, limit, cuts=(), held_as=jnp.bfloat16):
    values = spread * jax.random.normal(rng, extent, jnp.float32)
    if cuts:
        values = values * block_levels(rng, extent, cuts, -0.22, 0.18)
    return jnp.clip(values, -limit, limit).astype(held_as)


def setup_inputs(seed: int = 0, part: int = 0) -> dict:
    arg_keys = jax.random.split(jax.random.key(seed), 15)
    part_splits = jax.random.split(jax.random.fold_in(arg_keys[14], part), 15)
    latent = scatter_about(part_splits[0], (H1, C1, W1), 1.0, 6.0, ((0, 16), (1, 2)))
    cache_low_a = scatter_about(part_splits[1], (2, H1, C1, W1), 1.0, 6.0, ((1, 16), (2, 2)))
    cache_low_b = scatter_about(part_splits[2], (2, H1, C1, W1), 1.0, 6.0, ((1, 16), (2, 2)))
    gain_low_a = jnp.clip(0.5 + 1.0 * jax.random.uniform(arg_keys[3], (C1,), jnp.float32) ** block_levels(arg_keys[3], (C1,), ((0, 2),), -0.2, 0.2), 0.5, 1.5).astype(jnp.bfloat16)
    gain_low_b = jnp.clip(0.5 + 1.0 * jax.random.uniform(arg_keys[4], (C1,), jnp.float32) ** block_levels(arg_keys[4], (C1,), ((0, 2),), -0.2, 0.2), 0.5, 1.5).astype(jnp.bfloat16)
    kernel_low_a = scatter_about(arg_keys[5], (3, 3, 3, C1, C1), (27 * C1) ** -0.5, 0.0625, ((3, 2),))
    kernel_low_b = scatter_about(arg_keys[6], (3, 3, 3, C1, C1), (27 * C1) ** -0.5, 0.0625, ((3, 2),))
    resample_kernel = scatter_about(arg_keys[7], (3, 3, C2, C1), (9 * C1) ** -0.5, 0.109375, ((2, 16),))
    gain_high_a = jnp.clip(jax.random.uniform(arg_keys[8], (C2,), jnp.float32, 0.5, 1.5), 0.5, 1.5).astype(jnp.bfloat16)
    gain_high_b = jnp.clip(jax.random.uniform(arg_keys[9], (C2,), jnp.float32, 0.5, 1.5), 0.5, 1.5).astype(jnp.bfloat16)
    kernel_high_a = scatter_about(arg_keys[10], (3, 3, 3, C2, C2), (27 * C2) ** -0.5, 0.078125, ((3, 16),))
    kernel_high_b = scatter_about(arg_keys[11], (3, 3, 3, C2, C2), (27 * C2) ** -0.5, 0.078125, ((3, 16),))
    cache_high_a = scatter_about(part_splits[12], (2, H2, C2, W2), 1.0, 6.0, ((1, 16), (3, 2)))
    cache_high_b = scatter_about(part_splits[13], (2, H2, C2, W2), 1.0, 6.0, ((1, 16), (3, 2)))
    return {"latent": latent, "cache_low_a": cache_low_a, "cache_low_b": cache_low_b, "gain_low_a": gain_low_a, "gain_low_b": gain_low_b, "kernel_low_a": kernel_low_a, "kernel_low_b": kernel_low_b, "resample_kernel": resample_kernel, "gain_high_a": gain_high_a, "gain_high_b": gain_high_b, "kernel_high_a": kernel_high_a, "kernel_high_b": kernel_high_b, "cache_high_a": cache_high_a, "cache_high_b": cache_high_b}


def norm_silu(inputs, gains):
    values = inputs.astype(jnp.float32)
    scaled = values * lax.rsqrt(lax.optimization_barrier(jnp.mean(values * values, axis=-1, keepdims=True)) + 1e-06) * gains.astype(jnp.float32)
    return (scaled * jax.nn.sigmoid(scaled)).astype(jnp.bfloat16)

def plane_conv(planes, kernel):
    return lax.conv_general_dilated(planes[None].astype(jnp.float32), kernel.astype(jnp.float32), (1, 1), ((1, 1), (1, 1)), dimension_numbers=('NHWC', 'HWIO', 'NHWC'), precision=lax.Precision.HIGHEST)[0]

def causal_conv(cached, living, kernel):
    frames = jnp.concatenate([cached, living[None]], axis=0)
    totals = plane_conv(frames[0], kernel[0])
    for offset in range(1, 3):
        totals = totals + plane_conv(frames[offset], kernel[offset])
    return totals

def reference(latent, cache_low_a, cache_low_b, gain_low_a, gain_low_b, kernel_low_a, kernel_low_b, resample_kernel, gain_high_a, gain_high_b, kernel_high_a, kernel_high_b, cache_high_a, cache_high_b):
    latent = jnp.transpose(latent, (0, 2, 1))
    cache_low_a = jnp.transpose(cache_low_a, (0, 1, 3, 2))
    cache_low_b = jnp.transpose(cache_low_b, (0, 1, 3, 2))
    cache_high_a = jnp.transpose(cache_high_a, (0, 1, 3, 2))
    cache_high_b = jnp.transpose(cache_high_b, (0, 1, 3, 2))
    kernel_low_a = jnp.transpose(kernel_low_a, (0, 1, 2, 4, 3))
    kernel_low_b = jnp.transpose(kernel_low_b, (0, 1, 2, 4, 3))
    kernel_high_a = jnp.transpose(kernel_high_a, (0, 1, 2, 4, 3))
    kernel_high_b = jnp.transpose(kernel_high_b, (0, 1, 2, 4, 3))
    resample_kernel = jnp.transpose(resample_kernel, (0, 1, 3, 2))
    middle_low = causal_conv(cache_low_a, norm_silu(latent, gain_low_a), kernel_low_a).astype(jnp.bfloat16)
    level_one = (latent.astype(jnp.float32) + causal_conv(cache_low_b, norm_silu(middle_low, gain_low_b), kernel_low_b)).astype(jnp.bfloat16)
    upsampled = jnp.repeat(jnp.repeat(level_one, 2, axis=0), 2, axis=1)
    resampled = plane_conv(upsampled, resample_kernel).astype(jnp.bfloat16)
    middle_high = causal_conv(cache_high_a, norm_silu(resampled, gain_high_a), kernel_high_a).astype(jnp.bfloat16)
    decoded = (resampled.astype(jnp.float32) + causal_conv(cache_high_b, norm_silu(middle_high, gain_high_b), kernel_high_b)).astype(jnp.bfloat16)
    return jnp.transpose(decoded, (0, 2, 1))
```

```python
import jax
import jax.numpy as jnp
from jax import lax
from jax.experimental import pallas as pl
from jax.experimental.pallas import tpu as pltpu
from jax.sharding import PartitionSpec as P

MESH = pl.DeviceIdType.MESH
BF = jnp.bfloat16
F32 = jnp.float32

R_LAT, R_GAIN, R_CA, R_CB, R_MID, R_CPK, R_PKA, R_PKB = 0, 1, 2, 4, 6, 7, 8, 9
R_HA, R_HB, R_H2A, R_H2B = 10, 12, 14, 16
R_TILE, R_PACK = 18, 23
R_Z = 28
R_W0, R_W1, R_W2, R_W3, R_W4 = 31, 35, 39, 43, 47
N_REMOTE = 49
L_LAT, L_CA, L_CB, L_WA, L_WB, L_STG, L_HA, L_HB, L_OUT, L_GAIN, L_GH, L_RST = range(12)
N_LOCAL = 12


def kernel(
    lat_h, ca_h, cb_h, gl_h, wa_h, wb_h, res_h, gh_h, ka_h, kb_h, cha_h, chb_h,
    out_h,
    latf, caf, cbf, glf, ghf, w1a, w1b, x1, acc, hsend, hrecv, midf,
    stg, rst, pst, zb, wh,
    cha, chb, x2, acc2, lv, lt, lpk, lpkr, xl, rsd, cpk, cpkr, pk, pkr, outv,
    ssem, rsem, lsem,
):
    v, r, c = lax.axis_index("views"), lax.axis_index("rows"), lax.axis_index("chan")
    y, k = v // 2, lax.rem(v, 2)
    x, zh = r // 4, lax.rem(r, 4)
    oc = 1 - c
    piece = 4 * k + y
    up, dn = lax.rem(r + 15, 16), lax.rem(r + 1, 16)
    xn, xp = lax.rem(r + 4, 16), lax.rem(r + 12, 16)
    xni, xpi = lax.rem(x + 1, 4), lax.rem(x + 3, 4)
    yn, yp = lax.rem(v + 2, 8), lax.rem(v + 6, 8)
    yni, ypi = lax.rem(y + 1, 4), lax.rem(y + 3, 4)
    ov = 2 * y + 1 - k
    zpeers = [4 * x + lax.rem(zh + d, 4) for d in (1, 2, 3)]
    partner = {"chan": oc}
    peers = (
        [partner, {"rows": up}, {"rows": dn}, {"rows": up, "chan": oc}, {"rows": dn, "chan": oc}]
        + [{"rows": z} for z in zpeers]
        + [{"rows": xn}, {"rows": xp}, {"views": yn}, {"views": yp}, {"views": ov}]
    )
    barrier = pltpu.get_barrier_semaphore()
    for peer in peers:
        pl.semaphore_signal(barrier, inc=1, device_id=peer, device_id_type=MESH)

    def local(src, dst, slot):
        return pltpu.make_async_copy(src, dst, lsem.at[slot])

    def remote(src, dst, slot, target):
        return pltpu.make_async_remote_copy(
            src_ref=src, dst_ref=dst, send_sem=ssem.at[slot], recv_sem=rsem.at[slot],
            device_id=target, device_id_type=MESH,
        )

    half = pl.ds(pl.multiple_of(c * 192, 64), 192)
    local_lat = local(lat_h, latf.at[:, half, :], L_LAT)
    local_lat.start()
    local_gain = local(gl_h, glf.at[c], L_GAIN)
    local_gain.start()
    local_gh = local(gh_h, ghf, L_GH)
    local_gh.start()
    local_rst = local(res_h, rst, L_RST)
    local_rst.start()

    @pl.when(jnp.logical_and(piece >= 2, piece < 5))
    def _():
        local(ka_h.at[:, lax.rem(piece + 1, 3)], stg, L_STG).start()

    @pl.when(jnp.logical_or(piece < 2, piece >= 5))
    def _():
        local(kb_h.at[:, lax.rem(piece + 1, 3)], stg, L_STG).start()

    def weight_copies(src, dst, slot):
        @pl.loop(0, 9)
        def _(n):
            t, i = n // 3, lax.rem(n, 3)
            for j in range(3):
                local(
                    src.at[t, i, j],
                    dst.at[t, pl.ds(pl.multiple_of(i * 192, 64), 192), j * 384 : (j + 1) * 384],
                    slot,
                ).start()

    weight_copies(wa_h, w1a, L_WA)
    local_ca = local(ca_h, caf.at[:, :, half, :], L_CA)
    local_ca.start()
    local_cb = local(cb_h, cbf.at[:, :, half, :], L_CB)
    local_cb.start()
    weight_copies(wb_h, w1b, L_WB)
    local_ha = local(cha_h, cha, L_HA)
    local_ha.start()
    local_hb = local(chb_h, chb, L_HB)
    local_hb.start()

    pl.semaphore_wait(barrier, len(peers))

    send_lat = remote(lat_h, latf.at[:, half, :], R_LAT, partner)
    send_lat.start()
    send_gain = remote(gl_h, glf.at[c], R_GAIN, partner)
    send_gain.start()

    pst[...] = jnp.zeros_like(pst)
    local_rst.wait()
    local(ka_h.at[:, 0], stg, L_STG).wait()

    @pl.when(piece == 0)
    def _():
        for b in range(5):
            w = 384 if b < 4 else 256
            pst[0:12, b * 384 : b * 384 + w] = rst[b // 3, b % 3, :, 0:w].astype(F32)

    @pl.when(piece == 1)
    def _():
        pst[0:12, 0:128] = rst[1, 1, :, 256:384].astype(F32)
        for b in range(5, 9):
            o = 128 + (b - 5) * 384
            pst[0:12, o : o + 384] = rst[b // 3, b % 3].astype(F32)

    @pl.when(piece >= 2)
    def _():
        for t in range(3):
            for j in range(3):
                o = (3 * t + j) * 192
                pst[0:12, o : o + 192] = stg[t, j].astype(F32)

    zrow = pl.ds(pl.multiple_of(zh * 16, 16), 16)
    zb[zrow, :] = pst[...].astype(BF)
    z_copies = [
        remote(zb.at[zrow, :], zb.at[zrow, :], R_Z + d, {"rows": zpeers[d]}) for d in range(3)
    ]
    for copy in z_copies:
        copy.start()

    lane = lax.broadcasted_iota(jnp.int32, (1, 256), 1)
    eye = (
        lax.broadcasted_iota(jnp.int32, (192, 192), 0)
        == lax.broadcasted_iota(jnp.int32, (192, 192), 1)
    )

    def to_column(row):
        return jnp.sum(jnp.where(eye, row, 0.0), axis=1, keepdims=True)

    def to_row(column):
        return jnp.sum(jnp.where(eye, column, 0.0), axis=0, keepdims=True)

    def act(values, gain):
        mean = jnp.mean(values * values, axis=0, keepdims=True)
        u = values * lax.rsqrt(mean + 1e-06) * gain
        return u / (1.0 + jnp.exp(-u))

    def shifted(values, left, right):
        j0 = jnp.where(lane == 0, left, pltpu.roll(values, 1, 1))
        j2 = jnp.where(lane == 255, right, pltpu.roll(values, 255, 1))
        return j0.astype(BF), j2.astype(BF)

    def low_gain(n):
        return jnp.concatenate([to_column(glf[h, n, 0:1, :]) for h in range(2)], axis=0)

    def build_low(values, t, row):
        j0, j2 = shifted(values, 0.0, 0.0)
        x1[t, row, 0:384, :] = j0
        x1[t, row, 384:768, :] = values.astype(BF)
        x1[t, row, 768:1152, :] = j2

    def dots_low(w, t):
        @pl.loop(0, 2)
        def _(row):
            total = jnp.dot(w[t], x1[t, row], preferred_element_type=F32)
            for i in range(3):
                acc[row + 2 - i] += total[i * 192 : (i + 1) * 192]

    def halo_copies(slot, base):
        return [
            remote(hsend.at[0], hrecv.at[base + 1], slot, {"rows": up}),
            remote(hsend.at[1], hrecv.at[base], slot + 1, {"rows": dn}),
        ]

    has_up = (r > 0).astype(F32)
    has_dn = (r < 15).astype(F32)

    acc[...] = jnp.zeros_like(acc)
    local_lat.wait()
    local_gain.wait()
    send_lat.wait_recv()
    send_gain.wait_recv()
    send_ca = [remote(ca_h.at[t], caf.at[t, :, half, :], R_CA + t, partner) for t in range(2)]
    for copy in send_ca:
        copy.start()
    gain = low_gain(0)

    @pl.loop(0, 2)
    def _(row):
        build_low(act(latf[row].astype(F32), gain), 2, row)

    local(w1a, w1a, L_WA).wait()
    dots_low(w1a, 2)

    for copy in z_copies:
        copy.wait_recv()
    rows48 = lax.broadcasted_iota(jnp.int32, (48, 64), 0)
    cols64 = lax.broadcasted_iota(jnp.int32, (48, 64), 1)
    pick = jnp.logical_and(rows48 == 12 * (cols64 // 16) + cols64 % 16, cols64 % 16 < 12)
    own48 = pl.ds(pl.multiple_of(x * 48, 16), 48)
    wh[piece, own48, :] = jnp.dot(
        jnp.where(pick, 1.0, 0.0).astype(BF), zb[...], preferred_element_type=F32
    ).astype(BF)

    def rows_of(xi):
        return pl.ds(pl.multiple_of(xi * 48, 16), 48)

    own4 = pl.ds(4 * k, 4)

    def same(ref, slot, target):
        return remote(ref, ref, slot, target)

    to_xn, to_xp, to_yn, to_yp = {"rows": xn}, {"rows": xp}, {"views": yn}, {"views": yp}
    w0 = [
        same(wh.at[piece, own48, 0:896], R_W0, to_xn),
        same(wh.at[piece, own48, 0:896], R_W0 + 1, to_xp),
        same(wh.at[piece, own48, 896:1792], R_W0 + 2, to_yn),
        same(wh.at[piece, own48, 896:1792], R_W0 + 3, to_yp),
    ]
    w1 = [
        same(wh.at[piece, rows_of(xpi), 0:512], R_W1, to_xn),
        same(wh.at[piece, rows_of(xni), 512:896], R_W1 + 1, to_xp),
        same(wh.at[4 * k + ypi, own48, 896:1408], R_W1 + 2, to_yn),
        same(wh.at[4 * k + yni, own48, 1408:1792], R_W1 + 3, to_yp),
    ]
    w2 = [
        same(wh.at[piece, :, 0:896], R_W2, to_yn),
        same(wh.at[piece, :, 0:896], R_W2 + 1, to_yp),
        same(wh.at[own4, own48, 896:1792], R_W2 + 2, to_xn),
        same(wh.at[own4, own48, 896:1792], R_W2 + 3, to_xp),
    ]
    w3 = [
        same(wh.at[4 * k + ypi, :, 0:512], R_W3, to_yn),
        same(wh.at[4 * k + yni, :, 512:896], R_W3 + 1, to_yp),
        same(wh.at[own4, rows_of(xpi), 896:1408], R_W3 + 2, to_xn),
        same(wh.at[own4, rows_of(xni), 1408:1792], R_W3 + 3, to_xp),
    ]
    w4 = [
        same(wh.at[own4, :, 0:896], R_W4, {"views": ov}),
        same(wh.at[own4, :, 896:1792], R_W4 + 1, {"views": ov}),
    ]

    def advance(done, begun):
        for copy in done:
            copy.wait_recv()
        for copy in begun:
            copy.start()

    advance([], w0)

    local_ha.wait()
    local_hb.wait()

    def edge_of(values):
        return to_row(jnp.where(c == 0, values[:, 255:256], values[:, 0:1]))

    for n, frames in enumerate((cha, chb)):
        @pl.loop(0, 8)
        def _(m, n=n, frames=frames):
            cpk[pl.ds(8 * n + m, 1), :] = edge_of(frames[m // 4, lax.rem(m, 4)].astype(F32))

    send_cpk = remote(cpk, cpkr, R_CPK, partner)
    send_cpk.start()

    advance(w0, w1)

    local_ca.wait()
    for t in range(2):
        send_ca[t].wait_recv()
    send_cb = [remote(cb_h.at[t], cbf.at[t, :, half, :], R_CB + t, partner) for t in range(2)]
    for copy in send_cb:
        copy.start()

    @pl.loop(0, 4)
    def _(n):
        t, row = n // 2, lax.rem(n, 2)
        build_low(caf[t, row].astype(F32), t, row)

    for t in range(2):
        dots_low(w1a, t)

    hsend[0] = acc[0].astype(BF)
    hsend[1] = acc[3].astype(BF)
    halo_a = halo_copies(R_HA, 0)
    for copy in halo_a:
        copy.start()
    advance(w1, w2)
    for copy in halo_a:
        copy.wait_recv()
    midf[0, half, :] = (acc[1] + has_up * hrecv[0].astype(F32)).astype(BF)
    midf[1, half, :] = (acc[2] + has_dn * hrecv[1].astype(F32)).astype(BF)
    send_mid = remote(midf.at[:, half, :], midf.at[:, half, :], R_MID, partner)
    send_mid.start()

    acc[...] = jnp.zeros_like(acc)
    local_cb.wait()
    for t in range(2):
        send_cb[t].wait_recv()

    @pl.loop(0, 4)
    def _(n):
        t, row = n // 2, lax.rem(n, 2)
        build_low(cbf[t, row].astype(F32), t, row)

    local(w1b, w1b, L_WB).wait()
    for t in range(2):
        dots_low(w1b, t)

    send_mid.wait_recv()
    gain = low_gain(1)

    @pl.loop(0, 2)
    def _(row):
        build_low(act(midf[row].astype(F32), gain), 2, row)

    dots_low(w1b, 2)
    for copy in halo_a:
        copy.wait_send()
    hsend[0] = acc[0].astype(BF)
    hsend[1] = acc[3].astype(BF)
    halo_b = halo_copies(R_HB, 2)
    for copy in halo_b:
        copy.start()
    advance(w2, w3)

    send_cpk.wait_recv()
    is0, is1 = (c == 0).astype(F32), (c == 1).astype(F32)

    def build_high(values, margin, t, row):
        j0, j2 = shifted(values, margin * is1, margin * is0)
        base = t * 576
        x2[row, pl.ds(base, 192), :] = j0
        x2[row, pl.ds(base + 192, 192), :] = values.astype(BF)
        x2[row, pl.ds(base + 384, 192), :] = j2

    def cached_high(frames, n):
        for t in range(2):
            @pl.loop(0, 4)
            def _(row, t=t):
                margin = to_column(cpkr[pl.ds(8 * n + 4 * t + row, 1), :])
                build_high(frames[t, row].astype(F32), margin, t, row)

    def cached_dots(first):
        @pl.loop(0, 4)
        def _(row):
            total = jnp.dot(
                wh[first : first + 3, :, 0:1152].reshape(576, 1152), x2[row, 0:1152, :],
                preferred_element_type=F32,
            )
            for i in range(3):
                acc2[row + 2 - i] += total[i * 192 : (i + 1) * 192]

    def living_dots(first):
        @pl.loop(0, 4)
        def _(row):
            total = jnp.dot(
                wh[first : first + 3, :, 1152:1792].reshape(576, 640), x2[row, 1152:1792, :],
                preferred_element_type=F32,
            )
            for i in range(3):
                acc2[row + 2 - i] += total[i * 192 : (i + 1) * 192]

    for row in range(4):
        x2[row, 1728:1792, :] = jnp.zeros((64, 256), BF)
    acc2[...] = jnp.zeros_like(acc2)
    cached_high(cha, 0)

    for copy in halo_b:
        copy.wait_recv()
    for n, (scale, row) in enumerate(((has_up, 1), (has_dn, 2))):
        lv[n] = (
            latf[n, half, :].astype(F32) + (acc[row] + scale * hrecv[2 + n].astype(F32))
        ).astype(BF)

    chalf = pl.ds(pl.multiple_of(c * 128, 128), 128)
    ohalf = pl.ds(pl.multiple_of(oc * 128, 128), 128)
    for n in range(2):
        values = lv[n].astype(F32)
        lpk[2 * n : 2 * n + 1, :] = to_row(values[:, 127:128])
        lpk[2 * n + 1 : 2 * n + 2, :] = to_row(values[:, 128:129])
    tiles = [
        remote(lv.at[:, :, ohalf], lt.at[pl.ds(1, 2), half, :], R_TILE, partner),
        remote(lv.at[0, :, chalf], lt.at[3, half, :], R_TILE + 1, {"rows": up}),
        remote(lv.at[1, :, chalf], lt.at[0, half, :], R_TILE + 2, {"rows": dn}),
        remote(lv.at[0, :, ohalf], lt.at[3, half, :], R_TILE + 3, {"rows": up, "chan": oc}),
        remote(lv.at[1, :, ohalf], lt.at[0, half, :], R_TILE + 4, {"rows": dn, "chan": oc}),
    ]
    packs = [
        remote(lpk, lpkr.at[n], R_PACK + n, peers[n]) for n in range(5)
    ]
    for copy in packs + tiles:
        copy.start()
    lt[1, half, :] = lv[0, :, chalf]
    lt[2, half, :] = lv[1, :, chalf]
    advance(w3, w4)
    for copy in packs + tiles:
        copy.wait_recv()

    k128 = lax.broadcasted_iota(jnp.int32, (128, 256), 0)
    s256 = lax.broadcasted_iota(jnp.int32, (128, 256), 1)
    spread = [jnp.where(k128 == (s256 + j + 1) // 2 - 1, 1.0, 0.0).astype(BF) for j in range(3)]
    is_c0 = c == 0
    for slot in range(4):
        if slot in (1, 2):
            n = 2 * (slot - 1)
            mine, other = lpk[n : n + 2, :], lpkr[0, n : n + 2, :]
        elif slot == 0:
            mine, other = lpkr[2, 2:4, :], lpkr[4, 2:4, :]
        else:
            mine, other = lpkr[1, 0:2, :], lpkr[3, 0:2, :]
        mine = to_column(jnp.where(is_c0, mine[1:2], mine[0:1]))
        other = to_column(jnp.where(is_c0, other[1:2], other[0:1]))
        margin = jnp.concatenate(
            [jnp.where(is_c0, mine, other), jnp.where(is_c0, other, mine)], axis=0
        )
        scale = has_up if slot == 0 else has_dn if slot == 3 else 1.0
        margin = margin * scale
        tile = lt[slot]
        for j in range(3):
            wide = jnp.dot(tile, spread[j], preferred_element_type=F32) * scale
            if j == 0:
                wide = jnp.where(lane == 0, margin * is1, wide)
            if j == 2:
                wide = jnp.where(lane == 255, margin * is0, wide)
            xl[slot, j * 384 : (j + 1) * 384, :] = wide.astype(BF)

    for copy in w4:
        copy.wait_recv()

    local_gh.wait()
    gain2 = to_column(ghf[0, 0:1, :])

    for slot in range(4):
        for i in range(3):
            rows_out = [u for u in range(4) if (u + i + 1) // 2 == slot]
            if not rows_out:
                continue
            if i == 0:
                total = jnp.dot(wh[0, :, 0:1152], xl[slot], preferred_element_type=F32)
            elif i == 1:
                total = jnp.dot(wh[0, :, 1152:1792], xl[slot, 0:640, :], preferred_element_type=F32)
                total += jnp.dot(wh[1, :, 0:512], xl[slot, 640:1152, :], preferred_element_type=F32)
            else:
                total = jnp.dot(wh[1, :, 512:1664], xl[slot], preferred_element_type=F32)
            for u in rows_out:
                if slot == (u + 1) // 2 and i == 0:
                    outv[u] = total
                else:
                    outv[u] += total

    def living_high(value_of, gain, pack_slot, n):
        @pl.loop(0, 4)
        def _(row):
            values = act(value_of(row), gain)
            outv[row] = values
            pk[n, pl.ds(row, 1), :] = edge_of(values)

        send = remote(pk.at[n], pkr.at[n], pack_slot, partner)
        send.start()
        return send

    def finish_living(send, n):
        send.wait_recv()

        @pl.loop(0, 4)
        def _(row):
            build_high(outv[row], to_column(pkr[n, pl.ds(row, 1), :]), 2, row)

    def round_resampled(row):
        values = outv[row].astype(BF)
        rsd[row] = values
        return values.astype(F32)

    send_a = living_high(round_resampled, gain2, R_PKA, 0)
    cached_dots(2)
    finish_living(send_a, 0)
    living_dots(2)
    for copy in halo_b:
        copy.wait_send()
    hsend[0] = acc2[0].astype(BF)
    hsend[1] = acc2[5].astype(BF)

    halo_2a = halo_copies(R_H2A, 4)
    for copy in halo_2a:
        copy.start()
    for row in range(4):
        outv[row] = acc2[row + 1]

    acc2[...] = jnp.zeros_like(acc2)
    cached_high(chb, 1)
    cached_dots(5)
    for copy in halo_2a:
        copy.wait_recv()
    outv[0] += has_up * hrecv[4].astype(F32)
    outv[3] += has_dn * hrecv[5].astype(F32)

    gain2 = to_column(ghf[1, 0:1, :])
    send_b = living_high(lambda row: outv[row].astype(BF).astype(F32), gain2, R_PKB, 1)
    finish_living(send_b, 1)
    living_dots(5)
    for copy in halo_2a:
        copy.wait_send()
    hsend[0] = acc2[0].astype(BF)
    hsend[1] = acc2[5].astype(BF)
    halo_2b = halo_copies(R_H2B, 6)
    for copy in halo_2b:
        copy.start()
    for row in range(1, 3):
        rsd[row] = (rsd[row].astype(F32) + acc2[row + 1]).astype(BF)
    for copy in halo_2b:
        copy.wait_recv()
    rsd[0] = (rsd[0].astype(F32) + (acc2[1] + has_up * hrecv[6].astype(F32))).astype(BF)
    rsd[3] = (rsd[3].astype(F32) + (acc2[4] + has_dn * hrecv[7].astype(F32))).astype(BF)
    write = local(rsd, out_h, L_OUT)
    write.start()

    sends = (
        [send_lat, send_gain, send_cpk, send_mid, send_a, send_b]
        + send_ca + send_cb + z_copies + w0 + w1 + w2 + w3 + w4 + tiles + packs + halo_2b
    )
    for copy in sends:
        copy.wait_send()
    write.wait()


def body(
    latent, cache_low_a, cache_low_b, gain_low_a, gain_low_b, kernel_low_a, kernel_low_b,
    resample_kernel, gain_high_a, gain_high_b, kernel_high_a, kernel_high_b,
    cache_high_a, cache_high_b,
):
    def rows8(a, b):
        pair = jnp.stack([a, b]).astype(F32)
        return jnp.broadcast_to(pair[:, None, :], (2, 8, pair.shape[1]))

    gains_low = rows8(gain_low_a, gain_low_b)
    gains_high = rows8(gain_high_a, gain_high_b)
    vm = pltpu.VMEM
    return pl.pallas_call(
        kernel,
        out_shape=jax.ShapeDtypeStruct((4, 192, 256), BF),
        in_specs=[pl.BlockSpec(memory_space=pl.ANY)] * 12,
        out_specs=pl.BlockSpec(memory_space=pl.ANY),
        scratch_shapes=[
            vm((2, 384, 256), BF),
            vm((2, 2, 384, 256), BF),
            vm((2, 2, 384, 256), BF),
            vm((2, 2, 8, 192), F32),
            vm((2, 8, 192), F32),
            vm((3, 576, 1152), BF),
            vm((3, 576, 1152), BF),
            vm((3, 2, 1152, 256), BF),
            vm((4, 192, 256), F32),
            vm((2, 192, 256), BF),
            vm((8, 192, 256), BF),
            vm((2, 384, 256), BF),
            vm((3, 3, 12, 192), BF),
            vm((3, 3, 12, 384), BF),
            vm((16, 1792), F32),
            vm((64, 1792), BF),
            vm((8, 192, 1792), BF),
            vm((2, 4, 192, 256), BF),
            vm((2, 4, 192, 256), BF),
            vm((4, 1792, 256), BF),
            vm((6, 192, 256), F32),
            vm((2, 192, 256), BF),
            vm((4, 384, 128), BF),
            vm((8, 192), F32),
            vm((5, 8, 192), F32),
            vm((4, 1152, 256), BF),
            vm((4, 192, 256), BF),
            vm((16, 192), F32),
            vm((16, 192), F32),
            vm((2, 8, 192), F32),
            vm((2, 8, 192), F32),
            vm((4, 192, 256), F32),
            pltpu.SemaphoreType.DMA((N_REMOTE,)),
            pltpu.SemaphoreType.DMA((N_REMOTE,)),
            pltpu.SemaphoreType.DMA((N_LOCAL,)),
        ],
        compiler_params=pltpu.CompilerParams(
            collective_id=0, has_side_effects=True, vmem_limit_bytes=58 * 1024 * 1024
        ),
    )(
        latent, cache_low_a, cache_low_b, gains_low, kernel_low_a, kernel_low_b,
        resample_kernel, gains_high, kernel_high_a, kernel_high_b, cache_high_a, cache_high_b,
    )


def solution(mesh):
    placed = (
        P(("views", "rows"), "chan", None),
        P(None, ("views", "rows"), "chan", None),
        P(None, ("views", "rows"), "chan", None),
        P("chan"),
        P("chan"),
        P(None, None, None, "chan", None),
        P(None, None, None, "chan", None),
        P(None, None, "rows", None),
        P(),
        P(),
        P(None, None, None, "rows", None),
        P(None, None, None, "rows", None),
        P(None, ("views", "rows"), None, "chan"),
        P(None, ("views", "rows"), None, "chan"),
    )
    return jax.shard_map(
        body,
        mesh=mesh,
        in_specs=placed,
        out_specs=P(("views", "rows"), None, "chan"),
        check_vma=False,
    )
```

```python
import jax
import jax.numpy as jnp
from jax import lax
from jax.experimental import pallas as pl
from jax.experimental.pallas import tpu as pltpu
from jax.sharding import PartitionSpec as P

MESH = pl.DeviceIdType.MESH
BF = jnp.bfloat16
F32 = jnp.float32

R_LAT, R_GAIN, R_CA, R_CB, R_MID, R_CPK, R_PKA, R_PKB = 0, 49, 2, 4, 6, 7, 8, 9
R_HA, R_HB, R_H2A, R_H2B = 10, 12, 14, 16
R_TILE, R_PACK = 18, 23
R_Z = 28
R_W0, R_W1, R_W2, R_W3, R_W4 = 31, 35, 39, 43, 47
N_REMOTE = 51
L_LAT, L_CA, L_CB, L_WA, L_WB, L_STG, L_HA, L_HB, L_OUT, L_RST, L_GAIN = range(11)
N_LOCAL = 14


def kernel(
    lat_h, ca_h, cb_h, gla_h, glb_h, wa_h, wb_h, res_h, gha_h, ghb_h, ka_h, kb_h, cha_h, chb_h,
    out_h,
    latf, caf, cbf, gla, glao, glb, glbo, gha, ghb, w1a, w1b, x1, acc, hsend, hrecv, midf,
    stg, rst, pst, zb, zc, wh,
    cha, chb, x2, acc2, lv, lt, lpk, lpkr, xl, rsd, cpk, cpkr, columns, pk, pkr, outv,
    ssem, rsem, lsem,
):
    v, r, c = lax.axis_index("views"), lax.axis_index("rows"), lax.axis_index("chan")
    y, k = v // 2, lax.rem(v, 2)
    x, zh = r // 4, lax.rem(r, 4)
    oc = 1 - c
    piece = 4 * k + y
    up, dn = lax.rem(r + 15, 16), lax.rem(r + 1, 16)
    xn, xp = lax.rem(r + 4, 16), lax.rem(r + 12, 16)
    xni, xpi = lax.rem(x + 1, 4), lax.rem(x + 3, 4)
    yn, yp = lax.rem(v + 2, 8), lax.rem(v + 6, 8)
    yni, ypi = lax.rem(y + 1, 4), lax.rem(y + 3, 4)
    ov = 2 * y + 1 - k
    z_near, z_far = 4 * x + lax.rem(zh + 3 + 2 * c, 4), 4 * x + lax.rem(zh + 2, 4)
    z_targets = [
        {"rows": z_near, "chan": 0}, {"rows": z_near, "chan": 1}, {"rows": z_far, "chan": oc}
    ]
    z_sources = [
        {"rows": 4 * x + lax.rem(zh + 3, 4), "chan": 1},
        {"rows": 4 * x + lax.rem(zh + 1, 4), "chan": 0},
        {"rows": z_far, "chan": oc},
    ]
    partner = {"chan": oc}
    peers = (
        [partner, {"rows": up}, {"rows": dn}, {"rows": up, "chan": oc}, {"rows": dn, "chan": oc}]
        + z_sources
        + [{"rows": xn}, {"rows": xp}, {"views": yn}, {"views": yp}, {"views": ov}]
    )
    barrier = pltpu.get_barrier_semaphore()
    for peer in peers:
        pl.semaphore_signal(barrier, inc=1, device_id=peer, device_id_type=MESH)

    def local(src, dst, slot):
        return pltpu.make_async_copy(src, dst, lsem.at[slot])

    def remote(src, dst, slot, target, arrival=None):
        arrival = slot if arrival is None else arrival
        return pltpu.make_async_remote_copy(
            src_ref=src, dst_ref=dst, send_sem=ssem.at[slot], recv_sem=rsem.at[arrival],
            device_id=target, device_id_type=MESH,
        )

    half = pl.ds(pl.multiple_of(c * 192, 64), 192)
    local_lat = local(lat_h, latf.at[:, half, :], L_LAT)
    local_lat.start()
    local_gains = [
        local(src, dst, L_GAIN + n)
        for n, (src, dst) in enumerate(((gla_h, gla), (glb_h, glb), (gha_h, gha), (ghb_h, ghb)))
    ]
    for copy in local_gains:
        copy.start()
    local_rst = local(res_h, rst, L_RST)
    local_rst.start()

    @pl.when(jnp.logical_and(piece >= 2, piece < 5))
    def _():
        pltpu.make_async_copy(ka_h.at[:, lax.rem(piece + 1, 3)], stg, lsem.at[L_STG]).start()

    @pl.when(jnp.logical_or(piece < 2, piece >= 5))
    def _():
        pltpu.make_async_copy(kb_h.at[:, lax.rem(piece + 1, 3)], stg, lsem.at[L_STG]).start()

    def weight_copies(src, dst, slot):
        @pl.loop(0, 9)
        def _(n):
            t, i = n // 3, lax.rem(n, 3)
            for j in range(3):
                pltpu.make_async_copy(
                    src.at[t, i, j],
                    dst.at[t, pl.ds(pl.multiple_of(i * 192, 64), 192), j * 384 : (j + 1) * 384],
                    lsem.at[slot],
                ).start()

    pl.semaphore_wait(barrier, len(peers))

    send_lat = remote(lat_h, latf.at[:, half, :], R_LAT, partner)
    send_lat.start()
    send_gains = [remote(gla_h, glao, R_GAIN, partner), remote(glb_h, glbo, R_GAIN + 1, partner)]
    for copy in send_gains:
        copy.start()
    send_ca = [remote(ca_h.at[t], caf.at[t, :, half, :], R_CA + t, partner) for t in range(2)]
    for copy in send_ca:
        copy.start()

    weight_copies(wa_h, w1a, L_WA)
    low_a_here = local(w1a, w1a, L_WA)
    local_ca = local(ca_h, caf.at[:, :, half, :], L_CA)
    local_ca.start()
    local_cb = local(cb_h, cbf.at[:, :, half, :], L_CB)
    local_cb.start()
    weight_copies(wb_h, w1b, L_WB)
    low_b_here = local(w1b, w1b, L_WB)
    local_ha = local(cha_h, cha, L_HA)
    local_ha.start()
    local_hb = local(chb_h, chb, L_HB)
    local_hb.start()

    pst[...] = jnp.zeros_like(pst)
    local_rst.wait()
    local(ka_h.at[:, 0], stg, L_STG).wait()

    @pl.when(piece == 0)
    def _():
        for b in range(5):
            w = 384 if b < 4 else 256
            pst[0:12, b * 384 : b * 384 + w] = rst[b // 3, b % 3, :, 0:w].astype(F32)

    @pl.when(piece == 1)
    def _():
        pst[0:12, 0:128] = rst[1, 1, :, 256:384].astype(F32)
        for b in range(5, 9):
            o = 128 + (b - 5) * 384
            pst[0:12, o : o + 384] = rst[b // 3, b % 3].astype(F32)

    @pl.when(piece >= 2)
    def _():
        for t in range(3):
            for j in range(3):
                o = (3 * t + j) * 192
                pst[0:12, o : o + 192] = stg[t, j].astype(F32)

    zb[zh] = pst[0:12, :].astype(BF)
    own12 = zb.at[zh]
    zc[...] = jnp.zeros_like(zc)
    z_copies = [
        remote(own12, own12, R_Z + d, z_targets[d], R_Z + (c if d < 2 else 2)) for d in range(3)
    ]
    for copy in z_copies:
        copy.start()

    lane = lax.broadcasted_iota(jnp.int32, (1, 256), 1)
    eye = (
        lax.broadcasted_iota(jnp.int32, (192, 192), 0)
        == lax.broadcasted_iota(jnp.int32, (192, 192), 1)
    )

    def to_column(row):
        return jnp.sum(jnp.where(eye, row, 0.0), axis=1, keepdims=True)

    def to_row(column):
        return jnp.sum(jnp.where(eye, column, 0.0), axis=0, keepdims=True)

    def act(values, gain):
        mean = jnp.mean(values * values, axis=0, keepdims=True)
        u = values * lax.rsqrt(mean + 1e-06) * gain
        u = 0.5 * u
        return u + u * jnp.tanh(u)

    def shifted(values, left, right):
        j0 = jnp.where(lane == 0, left, pltpu.roll(values, 1, 1))
        j2 = jnp.where(lane == 255, right, pltpu.roll(values, 255, 1))
        return j0.astype(BF), j2.astype(BF)

    def column_of(ref):
        return to_column(ref[...].astype(F32).reshape(1, 192))

    def low_gain(own, other):
        own, other = column_of(own), column_of(other)
        return jnp.concatenate(
            [jnp.where(c == 0, own, other), jnp.where(c == 0, other, own)], axis=0
        )

    def build_low(values, t, row):
        j0, j2 = shifted(values, 0.0, 0.0)
        x1[t, row, 0:384, :] = j0
        x1[t, row, 384:768, :] = values.astype(BF)
        x1[t, row, 768:1152, :] = j2

    def dots_low(w, t):
        @pl.loop(0, 2)
        def _(row):
            total = jnp.dot(w[t], x1[t, row], preferred_element_type=F32)
            for i in range(3):
                acc[row + 2 - i] += total[i * 192 : (i + 1) * 192]

    def halo_low(w, frames):
        for t in frames:
            acc[0] += jnp.dot(w[t, 384:576], x1[t, 0], preferred_element_type=F32)
            acc[3] += jnp.dot(w[t, 0:192], x1[t, 1], preferred_element_type=F32)

    def inner_low(w, t):
        total = jnp.dot(w[t, 0:384], x1[t, 0], preferred_element_type=F32)
        acc[2] += total[0:192]
        acc[1] += total[192:384]
        total = jnp.dot(w[t, 192:576], x1[t, 1], preferred_element_type=F32)
        acc[2] += total[0:192]
        acc[1] += total[192:384]

    def halo_copies(slot, base):
        return [
            remote(hsend.at[0], hrecv.at[base + 1], slot, {"rows": up}),
            remote(hsend.at[1], hrecv.at[base], slot + 1, {"rows": dn}),
        ]

    has_up = (r > 0).astype(F32)
    has_dn = (r < 15).astype(F32)

    acc[...] = jnp.zeros_like(acc)
    local_lat.wait()
    for copy in local_gains:
        copy.wait()
    send_lat.wait_recv()
    for copy in send_gains:
        copy.wait_recv()
    gain = low_gain(gla, glao)

    @pl.loop(0, 2)
    def _(row):
        build_low(act(latf[row].astype(F32), gain), 2, row)

    low_a_here.wait()
    dots_low(w1a, 2)

    for d in range(3):
        remote(own12, own12, R_Z + d, z_targets[d]).wait_recv()
    for n in range(4):
        zc[16 * n : 16 * n + 12, :] = zb[n]
    rows48 = lax.broadcasted_iota(jnp.int32, (48, 64), 0)
    cols64 = lax.broadcasted_iota(jnp.int32, (48, 64), 1)
    pick = jnp.logical_and(rows48 == 12 * (cols64 // 16) + cols64 % 16, cols64 % 16 < 12)
    own48 = pl.ds(pl.multiple_of(x * 48, 16), 48)
    wh[piece, own48, :] = jnp.dot(
        jnp.where(pick, 1.0, 0.0).astype(BF), zc[...], preferred_element_type=F32
    ).astype(BF)

    def rows_of(xi):
        return pl.ds(pl.multiple_of(xi * 48, 16), 48)

    own4 = pl.ds(4 * k, 4)

    def same(ref, slot, target):
        return remote(ref, ref, slot, target)

    to_xn, to_xp, to_yn, to_yp = {"rows": xn}, {"rows": xp}, {"views": yn}, {"views": yp}
    w0 = [
        same(wh.at[piece, own48, 0:896], R_W0, to_xn),
        same(wh.at[piece, own48, 0:896], R_W0 + 1, to_xp),
        same(wh.at[piece, own48, 896:1792], R_W0 + 2, to_yn),
        same(wh.at[piece, own48, 896:1792], R_W0 + 3, to_yp),
    ]
    w1 = [
        same(wh.at[piece, rows_of(xpi), 0:512], R_W1, to_xn),
        same(wh.at[piece, rows_of(xni), 512:896], R_W1 + 1, to_xp),
        same(wh.at[4 * k + ypi, own48, 896:1408], R_W1 + 2, to_yn),
        same(wh.at[4 * k + yni, own48, 1408:1792], R_W1 + 3, to_yp),
    ]
    w2 = [
        same(wh.at[piece, :, 0:896], R_W2, to_yn),
        same(wh.at[piece, :, 0:896], R_W2 + 1, to_yp),
        same(wh.at[own4, own48, 896:1792], R_W2 + 2, to_xn),
        same(wh.at[own4, own48, 896:1792], R_W2 + 3, to_xp),
    ]
    w3 = [
        same(wh.at[4 * k + ypi, :, 0:512], R_W3, to_yn),
        same(wh.at[4 * k + yni, :, 512:896], R_W3 + 1, to_yp),
        same(wh.at[own4, rows_of(xpi), 896:1408], R_W3 + 2, to_xn),
        same(wh.at[own4, rows_of(xni), 1408:1792], R_W3 + 3, to_xp),
    ]
    w4 = [
        same(wh.at[own4, :, 0:896], R_W4, {"views": ov}),
        same(wh.at[own4, :, 896:1792], R_W4 + 1, {"views": ov}),
    ]

    def advance(done, begun):
        for copy in done:
            copy.wait_recv()
        for copy in begun:
            copy.start()

    advance([], w0)

    local_ha.wait()
    local_hb.wait()

    lane128 = lax.broadcasted_iota(jnp.int32, (1, 128), 1)
    edge_tile = pl.ds(pl.multiple_of((1 - c) * 128, 128), 128)

    def put_edge(pack, tile, m):
        return jnp.where(lane128 == m, pltpu.roll(tile, m + 1 - c, 1), pack)

    edges = jnp.zeros((192, 128), F32)
    for n, frames in enumerate((cha, chb)):
        for m in range(8):
            edges = put_edge(edges, frames[m // 4, m % 4, :, edge_tile].astype(F32), 8 * n + m)
    cpk[...] = edges.T[0:16]

    send_cpk = remote(cpk, cpkr.at[0:16], R_CPK, partner)
    send_cpk.start()

    advance(w0, w1)

    local_ca.wait()
    for t in range(2):
        send_ca[t].wait_recv()
    send_cb = [remote(cb_h.at[t], cbf.at[t, :, half, :], R_CB + t, partner) for t in range(2)]
    send_cb[0].start()
    @pl.loop(0, 4)
    def _(n):
        t, row = n // 2, lax.rem(n, 2)
        build_low(caf[t, row].astype(F32), t, row)

    halo_low(w1a, (0, 1))
    hsend[0] = acc[0].astype(BF)
    hsend[1] = acc[3].astype(BF)
    halo_a = halo_copies(R_HA, 0)
    for copy in halo_a:
        copy.start()
    for t in range(2):
        inner_low(w1a, t)
    for copy in halo_a:
        copy.wait_send()
    send_cb[1].start()
    advance(w1, w2)
    for copy in halo_a:
        copy.wait_recv()
    midf[0, half, :] = (acc[1] + has_up * hrecv[0].astype(F32)).astype(BF)
    midf[1, half, :] = (acc[2] + has_dn * hrecv[1].astype(F32)).astype(BF)
    send_mid = remote(midf.at[:, half, :], midf.at[:, half, :], R_MID, partner)
    send_mid.start()

    acc[...] = jnp.zeros_like(acc)
    local_cb.wait()
    for t in range(2):
        send_cb[t].wait_recv()

    @pl.loop(0, 4)
    def _(n):
        t, row = n // 2, lax.rem(n, 2)
        build_low(cbf[t, row].astype(F32), t, row)

    low_b_here.wait()
    for t in range(2):
        dots_low(w1b, t)

    send_mid.wait_recv()
    gain = low_gain(glb, glbo)

    @pl.loop(0, 2)
    def _(row):
        build_low(act(midf[row].astype(F32), gain), 2, row)

    halo_low(w1b, (2,))
    hsend[0] = acc[0].astype(BF)
    hsend[1] = acc[3].astype(BF)
    halo_b = halo_copies(R_HB, 2)
    for copy in halo_b:
        copy.start()
    inner_low(w1b, 2)
    advance(w2, w3)

    send_cpk.wait_recv()
    is0, is1 = (c == 0).astype(F32), (c == 1).astype(F32)
    columns[...] = cpkr[...].T

    def build_high(values, margins, m, t, row):
        left = pltpu.roll(margins, lax.rem(128 - m, 128), 1) * is1
        right = pltpu.roll(margins, 127 - m, 1) * is0
        sides = jnp.concatenate([left, right], axis=1)
        j0, j2 = shifted(values, sides, sides)
        base = t * 576
        x2[row, pl.ds(base, 192), :] = j0
        x2[row, pl.ds(base + 192, 192), :] = values.astype(BF)
        x2[row, pl.ds(base + 384, 192), :] = j2

    def cached_high(frames, n):
        margins = columns[...]
        for t in range(2):
            @pl.loop(0, 4)
            def _(row, t=t):
                build_high(frames[t, row].astype(F32), margins, 8 * n + 4 * t + row, t, row)

    def cached_dots(first):
        @pl.loop(0, 4)
        def _(row):
            total = jnp.dot(
                wh[first : first + 3, :, 0:1152].reshape(576, 1152), x2[row, 0:1152, :],
                preferred_element_type=F32,
            )
            for i in range(3):
                acc2[row + 2 - i] += total[i * 192 : (i + 1) * 192]

    def halo_high(first):
        acc2[0] += jnp.dot(
            wh[first + 2, :, 1152:1792], x2[0, 1152:1792, :], preferred_element_type=F32
        )
        acc2[5] += jnp.dot(wh[first, :, 1152:1792], x2[3, 1152:1792, :], preferred_element_type=F32)
        hsend[0] = acc2[0].astype(BF)
        hsend[1] = acc2[5].astype(BF)

    def inner_high(first):
        @pl.loop(1, 3)
        def _(row):
            total = jnp.dot(
                wh[first : first + 3, :, 1152:1792].reshape(576, 640), x2[row, 1152:1792, :],
                preferred_element_type=F32,
            )
            for i in range(3):
                acc2[row + 2 - i] += total[i * 192 : (i + 1) * 192]

        for row, low in ((0, 0), (3, 1)):
            total = jnp.dot(
                wh[first + low : first + low + 2, :, 1152:1792].reshape(384, 640),
                x2[row, 1152:1792, :], preferred_element_type=F32,
            )
            acc2[row + 2 - low] += total[0:192]
            acc2[row + 1 - low] += total[192:384]

    for row in range(4):
        x2[row, 1728:1792, :] = jnp.zeros((64, 256), BF)
    acc2[...] = jnp.zeros_like(acc2)
    cached_high(cha, 0)

    for copy in halo_b:
        copy.wait_recv()
    for n, (scale, row) in enumerate(((has_up, 1), (has_dn, 2))):
        lv[n] = (
            latf[n, half, :].astype(F32) + (acc[row] + scale * hrecv[2 + n].astype(F32))
        ).astype(BF)

    chalf = pl.ds(pl.multiple_of(c * 128, 128), 128)
    ohalf = pl.ds(pl.multiple_of(oc * 128, 128), 128)
    for n in range(2):
        values = lv[n].astype(F32)
        lpk[2 * n : 2 * n + 1, :] = to_row(values[:, 127:128])
        lpk[2 * n + 1 : 2 * n + 2, :] = to_row(values[:, 128:129])
    tiles = [
        remote(lv.at[:, :, ohalf], lt.at[pl.ds(1, 2), half, :], R_TILE, partner),
        remote(lv.at[0, :, chalf], lt.at[3, half, :], R_TILE + 1, {"rows": up}),
        remote(lv.at[1, :, chalf], lt.at[0, half, :], R_TILE + 2, {"rows": dn}),
        remote(lv.at[0, :, ohalf], lt.at[3, half, :], R_TILE + 3, {"rows": up, "chan": oc}),
        remote(lv.at[1, :, ohalf], lt.at[0, half, :], R_TILE + 4, {"rows": dn, "chan": oc}),
    ]
    packs = [
        remote(lpk, lpkr.at[n], R_PACK + n, peers[n]) for n in range(5)
    ]
    for copy in packs + tiles:
        copy.start()
    lt[1, half, :] = lv[0, :, chalf]
    lt[2, half, :] = lv[1, :, chalf]
    advance(w3, w4)
    for copy in packs + tiles:
        copy.wait_recv()

    k128 = lax.broadcasted_iota(jnp.int32, (128, 256), 0)
    s256 = lax.broadcasted_iota(jnp.int32, (128, 256), 1)
    spread = [jnp.where(k128 == (s256 + j + 1) // 2 - 1, 1.0, 0.0).astype(BF) for j in range(3)]
    is_c0 = c == 0
    for slot in range(4):
        if slot in (1, 2):
            n = 2 * (slot - 1)
            mine, other = lpk[n : n + 2, :], lpkr[0, n : n + 2, :]
        elif slot == 0:
            mine, other = lpkr[2, 2:4, :], lpkr[4, 2:4, :]
        else:
            mine, other = lpkr[1, 0:2, :], lpkr[3, 0:2, :]
        mine = to_column(jnp.where(is_c0, mine[1:2], mine[0:1]))
        other = to_column(jnp.where(is_c0, other[1:2], other[0:1]))
        margin = jnp.concatenate(
            [jnp.where(is_c0, mine, other), jnp.where(is_c0, other, mine)], axis=0
        )
        scale = has_up if slot == 0 else has_dn if slot == 3 else 1.0
        margin = margin * scale
        tile = lt[slot]
        for j in range(3):
            wide = jnp.dot(tile, spread[j], preferred_element_type=F32) * scale
            if j == 0:
                wide = jnp.where(lane == 0, margin * is1, wide)
            if j == 2:
                wide = jnp.where(lane == 255, margin * is0, wide)
            xl[slot, j * 384 : (j + 1) * 384, :] = wide.astype(BF)

    for copy in w4:
        copy.wait_recv()

    gain2 = column_of(gha)

    for slot in range(4):
        for i in range(3):
            rows_out = [u for u in range(4) if (u + i + 1) // 2 == slot]
            if not rows_out:
                continue
            if i == 0:
                total = jnp.dot(wh[0, :, 0:1152], xl[slot], preferred_element_type=F32)
            elif i == 1:
                total = jnp.dot(wh[0, :, 1152:1792], xl[slot, 0:640, :], preferred_element_type=F32)
                total += jnp.dot(wh[1, :, 0:512], xl[slot, 640:1152, :], preferred_element_type=F32)
            else:
                total = jnp.dot(wh[1, :, 512:1664], xl[slot], preferred_element_type=F32)
            for u in rows_out:
                if slot == (u + 1) // 2 and i == 0:
                    outv[u] = total
                else:
                    outv[u] += total

    def living_high(value_of, gain, pack_slot, n):
        @pl.loop(0, 4)
        def _(row):
            values = act(value_of(row), gain)
            outv[row] = values

        edges = jnp.zeros((192, 128), F32)
        for row in range(4):
            edges = put_edge(edges, outv[row, :, edge_tile], row)
        pk[n] = edges.T[0:8]
        send = remote(pk.at[n], pkr.at[n, 0:8], pack_slot, partner)
        send.start()
        return send

    def finish_living(send, n):
        send.wait_recv()

        margins = pkr[n].T

        @pl.loop(0, 4)
        def _(row):
            build_high(outv[row], margins, row, 2, row)

    def round_resampled(row):
        values = outv[row].astype(BF)
        rsd[row] = values
        return values.astype(F32)

    send_a = living_high(round_resampled, gain2, R_PKA, 0)
    cached_dots(2)
    finish_living(send_a, 0)
    for copy in halo_b:
        copy.wait_send()
    halo_high(2)

    halo_2a = halo_copies(R_H2A, 4)
    for copy in halo_2a:
        copy.start()
    inner_high(2)
    for row in range(4):
        outv[row] = acc2[row + 1]

    acc2[...] = jnp.zeros_like(acc2)
    cached_high(chb, 1)
    cached_dots(5)
    for copy in halo_2a:
        copy.wait_recv()
    outv[0] += has_up * hrecv[4].astype(F32)
    outv[3] += has_dn * hrecv[5].astype(F32)

    gain2 = column_of(ghb)
    send_b = living_high(lambda row: outv[row].astype(BF).astype(F32), gain2, R_PKB, 1)
    finish_living(send_b, 1)
    for copy in halo_2a:
        copy.wait_send()
    halo_high(5)
    halo_2b = halo_copies(R_H2B, 6)
    for copy in halo_2b:
        copy.start()
    inner_high(5)
    for row in range(1, 3):
        rsd[row] = (rsd[row].astype(F32) + acc2[row + 1]).astype(BF)
    for copy in halo_2b:
        copy.wait_recv()
    rsd[0] = (rsd[0].astype(F32) + (acc2[1] + has_up * hrecv[6].astype(F32))).astype(BF)
    rsd[3] = (rsd[3].astype(F32) + (acc2[4] + has_dn * hrecv[7].astype(F32))).astype(BF)
    write = local(rsd, out_h, L_OUT)
    write.start()

    sends = (
        [send_lat, send_cpk, send_mid, send_a, send_b]
        + send_gains + send_ca + send_cb + z_copies + w0 + w1 + w2 + w3 + w4 + tiles + packs + halo_2b
    )
    for copy in sends:
        copy.wait_send()
    write.wait()


def body(
    latent, cache_low_a, cache_low_b, gain_low_a, gain_low_b, kernel_low_a, kernel_low_b,
    resample_kernel, gain_high_a, gain_high_b, kernel_high_a, kernel_high_b,
    cache_high_a, cache_high_b,
):
    vm = pltpu.VMEM
    return pl.pallas_call(
        kernel,
        out_shape=jax.ShapeDtypeStruct((4, 192, 256), BF),
        in_specs=[pl.BlockSpec(memory_space=pl.ANY)] * 14,
        out_specs=pl.BlockSpec(memory_space=pl.ANY),
        scratch_shapes=[
            vm((2, 384, 256), BF),
            vm((2, 2, 384, 256), BF),
            vm((2, 2, 384, 256), BF),
            vm((192,), BF),
            vm((192,), BF),
            vm((192,), BF),
            vm((192,), BF),
            vm((192,), BF),
            vm((192,), BF),
            vm((3, 576, 1152), BF),
            vm((3, 576, 1152), BF),
            vm((3, 2, 1152, 256), BF),
            vm((4, 192, 256), F32),
            vm((2, 192, 256), BF),
            vm((8, 192, 256), BF),
            vm((2, 384, 256), BF),
            vm((3, 3, 12, 192), BF),
            vm((3, 3, 12, 384), BF),
            vm((16, 1792), F32),
            vm((4, 12, 1792), BF),
            vm((64, 1792), BF),
            vm((8, 192, 1792), BF),
            vm((2, 4, 192, 256), BF),
            vm((2, 4, 192, 256), BF),
            vm((4, 1792, 256), BF),
            vm((6, 192, 256), F32),
            vm((2, 192, 256), BF),
            vm((4, 384, 128), BF),
            vm((8, 192), F32),
            vm((5, 8, 192), F32),
            vm((4, 1152, 256), BF),
            vm((4, 192, 256), BF),
            vm((16, 192), F32),
            vm((128, 192), F32),
            vm((192, 128), F32),
            vm((2, 8, 192), F32),
            vm((2, 128, 192), F32),
            vm((4, 192, 256), F32),
            pltpu.SemaphoreType.DMA((N_REMOTE,)),
            pltpu.SemaphoreType.DMA((N_REMOTE,)),
            pltpu.SemaphoreType.DMA((N_LOCAL,)),
        ],
        compiler_params=pltpu.CompilerParams(
            collective_id=0, has_side_effects=True, vmem_limit_bytes=58 * 1024 * 1024
        ),
    )(
        latent, cache_low_a, cache_low_b, gain_low_a, gain_low_b, kernel_low_a, kernel_low_b,
        resample_kernel, gain_high_a, gain_high_b, kernel_high_a, kernel_high_b, cache_high_a, cache_high_b,
    )


def solution(mesh):
    placed = (
        P(("views", "rows"), "chan", None),
        P(None, ("views", "rows"), "chan", None),
        P(None, ("views", "rows"), "chan", None),
        P("chan"),
        P("chan"),
        P(None, None, None, "chan", None),
        P(None, None, None, "chan", None),
        P(None, None, "rows", None),
        P(),
        P(),
        P(None, None, None, "rows", None),
        P(None, None, None, "rows", None),
        P(None, ("views", "rows"), None, "chan"),
        P(None, ("views", "rows"), None, "chan"),
    )
    return jax.shard_map(
        body,
        mesh=mesh,
        in_specs=placed,
        out_specs=P(("views", "rows"), None, "chan"),
        check_vma=False,
    )
```

```python
import jax
import jax.numpy as jnp
from jax import lax
from jax.experimental import pallas as pl
from jax.experimental.pallas import tpu as pltpu
from jax.sharding import PartitionSpec as P

MESH = pl.DeviceIdType.MESH
BF = jnp.bfloat16
F32 = jnp.float32

R_LAT, R_GAIN, R_CA, R_CB, R_MID, R_CPK, R_PKA, R_PKB = 0, 49, 2, 4, 6, 7, 8, 9
R_HA, R_HB, R_H2A, R_H2B = 10, 12, 14, 16
R_TILE, R_PACK = 18, 23
R_Z = 28
R_W0, R_W1, R_W2, R_W3, R_W4 = 31, 35, 39, 43, 47
N_REMOTE = 51
L_LAT, L_CA, L_CB, L_WA, L_WB, L_STG, L_HA, L_HB, L_OUT, L_RST, L_GAIN = range(11)
N_LOCAL = 14


def kernel(
    lat_h, ca_h, cb_h, gla_h, glb_h, wa_h, wb_h, res_h, gha_h, ghb_h, ka_h, kb_h, cha_h, chb_h,
    out_h,
    latf, caf, cbf, gla, glao, glb, glbo, gha, ghb, w1a, w1b, x1, acc, hsend, hrecv, midf,
    stg, rst, pst, zb, zc, wh,
    cha, chb, x2, acc2, lv, lt, lpk, lpkr, xl, rsd, cpk, cpkr, columns, pk, pkr, outv, x2l, esend, erecv,
    ssem, rsem, lsem, rounds,
):
    v, r, c = lax.axis_index("views"), lax.axis_index("rows"), lax.axis_index("chan")
    y, k = v // 2, lax.rem(v, 2)
    x, zh = r // 4, lax.rem(r, 4)
    oc = 1 - c
    piece = 4 * k + y
    up, dn = lax.rem(r + 15, 16), lax.rem(r + 1, 16)
    xn, xp = lax.rem(r + 4, 16), lax.rem(r + 12, 16)
    xni, xpi = lax.rem(x + 1, 4), lax.rem(x + 3, 4)
    yn, yp = lax.rem(v + 2, 8), lax.rem(v + 6, 8)
    yni, ypi = lax.rem(y + 1, 4), lax.rem(y + 3, 4)
    ov = 2 * y + 1 - k
    z_near, z_far = 4 * x + lax.rem(zh + 3 + 2 * c, 4), 4 * x + lax.rem(zh + 2, 4)
    z_targets = [
        {"rows": z_near, "chan": 0}, {"rows": z_near, "chan": 1}, {"rows": z_far, "chan": oc}
    ]
    partner = {"chan": oc}
    along = [partner, {"rows": z_near, "chan": oc}, {"rows": xn}, {"rows": xp}]
    peers = along + [{"views": yn}, {"views": yp}, {"views": ov}]
    around = [
        partner, {"rows": up}, {"rows": dn}, {"rows": up, "chan": oc}, {"rows": dn, "chan": oc}
    ]
    barrier = pltpu.get_barrier_semaphore()
    for peer in peers:
        pl.semaphore_signal(barrier, inc=1, device_id=peer, device_id_type=MESH)

    def local(src, dst, slot):
        return pltpu.make_async_copy(src, dst, lsem.at[slot])

    def remote(src, dst, slot, target, arrival=None):
        arrival = slot if arrival is None else arrival
        return pltpu.make_async_remote_copy(
            src_ref=src, dst_ref=dst, send_sem=ssem.at[slot], recv_sem=rsem.at[arrival],
            device_id=target, device_id_type=MESH,
        )

    half = pl.ds(pl.multiple_of(c * 192, 64), 192)
    local_lat = local(lat_h, latf.at[:, half, :], L_LAT)
    local_lat.start()
    local_gains = [
        local(src, dst, L_GAIN + n)
        for n, (src, dst) in enumerate(((gla_h, gla), (glb_h, glb), (gha_h, gha), (ghb_h, ghb)))
    ]
    for copy in local_gains:
        copy.start()
    local_rst = local(res_h, rst, L_RST)
    local_rst.start()

    @pl.when(jnp.logical_and(piece >= 2, piece < 5))
    def _():
        pltpu.make_async_copy(ka_h.at[:, lax.rem(piece + 1, 3)], stg, lsem.at[L_STG]).start()

    @pl.when(jnp.logical_or(piece < 2, piece >= 5))
    def _():
        pltpu.make_async_copy(kb_h.at[:, lax.rem(piece + 1, 3)], stg, lsem.at[L_STG]).start()

    def weight_copies(src, dst, slot):
        @pl.loop(0, 9)
        def _(n):
            t, i = n // 3, lax.rem(n, 3)
            for j in range(3):
                pltpu.make_async_copy(
                    src.at[t, i, j],
                    dst.at[t, pl.ds(pl.multiple_of(i * 192, 64), 192), j * 384 : (j + 1) * 384],
                    lsem.at[slot],
                ).start()

    pl.semaphore_wait(barrier, len(peers))

    send_lat = remote(lat_h, latf.at[:, half, :], R_LAT, partner)
    send_lat.start()
    send_gains = [remote(gla_h, glao, R_GAIN, partner), remote(glb_h, glbo, R_GAIN + 1, partner)]
    for copy in send_gains:
        copy.start()
    send_ca = [remote(ca_h.at[t], caf.at[t, :, half, :], R_CA + t, partner) for t in range(2)]
    for copy in send_ca:
        copy.start()

    def begin_round(n):
        for peer in along:
            pl.semaphore_signal(rounds.at[n], inc=1, device_id=peer, device_id_type=MESH)

    def end_round(n):
        pl.semaphore_wait(rounds.at[n], len(along))

    begin_round(0)
    weight_copies(wa_h, w1a, L_WA)
    low_a_here = local(w1a, w1a, L_WA)
    end_round(0)
    begin_round(1)
    pst[...] = jnp.zeros_like(pst)
    local_rst.wait()
    local(ka_h.at[:, 0], stg, L_STG).wait()

    @pl.when(piece == 0)
    def _():
        for b in range(5):
            w = 384 if b < 4 else 256
            pst[0:12, b * 384 : b * 384 + w] = rst[b // 3, b % 3, :, 0:w].astype(F32)

    @pl.when(piece == 1)
    def _():
        pst[0:12, 0:128] = rst[1, 1, :, 256:384].astype(F32)
        for b in range(5, 9):
            o = 128 + (b - 5) * 384
            pst[0:12, o : o + 384] = rst[b // 3, b % 3].astype(F32)

    @pl.when(piece >= 2)
    def _():
        for t in range(3):
            for j in range(3):
                o = (3 * t + j) * 192
                pst[0:12, o : o + 192] = stg[t, j].astype(F32)

    zb[zh] = pst[0:12, :].astype(BF)
    own12 = zb.at[zh]
    zc[...] = jnp.zeros_like(zc)
    z_copies = [
        remote(own12, own12, R_Z + d, z_targets[d], R_Z + (c if d < 2 else 2)) for d in range(3)
    ]
    end_round(1)
    begin_round(2)
    local_ca = local(ca_h, caf.at[:, :, half, :], L_CA)
    local_ca.start()
    local_ha = local(cha_h, cha, L_HA)
    local_ha.start()
    local_hb = local(chb_h, chb, L_HB)
    local_hb.start()
    end_round(2)
    for copy in z_copies:
        copy.start()
    local_cb = local(cb_h, cbf.at[:, :, half, :], L_CB)
    local_cb.start()
    weight_copies(wb_h, w1b, L_WB)
    low_b_here = local(w1b, w1b, L_WB)

    lane = lax.broadcasted_iota(jnp.int32, (1, 256), 1)
    eye = (
        lax.broadcasted_iota(jnp.int32, (192, 192), 0)
        == lax.broadcasted_iota(jnp.int32, (192, 192), 1)
    )

    def to_column(row):
        return jnp.sum(jnp.where(eye, row, 0.0), axis=1, keepdims=True)

    def to_row(column):
        return jnp.sum(jnp.where(eye, column, 0.0), axis=0, keepdims=True)

    def act(values, gain):
        mean = jnp.mean(values * values, axis=0, keepdims=True)
        u = values * lax.rsqrt(mean + 1e-06) * gain
        u = 0.5 * u
        return u + u * jnp.tanh(u)

    def shifted(values, left, right):
        values = values.astype(BF)
        left, right = (jnp.broadcast_to(side, values.shape).astype(BF) for side in (left, right))
        j0 = jnp.where(lane == 0, left, pltpu.roll(values, 1, 1))
        j2 = jnp.where(lane == 255, right, pltpu.roll(values, 255, 1))
        return j0, j2

    def column_of(ref):
        return to_column(ref[...].astype(F32).reshape(1, 192))

    def low_gain(own, other):
        own, other = column_of(own), column_of(other)
        return jnp.concatenate(
            [jnp.where(c == 0, own, other), jnp.where(c == 0, other, own)], axis=0
        )

    def build_low(values, t, row):
        j0, j2 = shifted(values, 0.0, 0.0)
        x1[t, row, 0:384, :] = j0
        x1[t, row, 384:768, :] = values.astype(BF)
        x1[t, row, 768:1152, :] = j2

    def dots_low(w, t):
        @pl.loop(0, 2)
        def _(row):
            total = jnp.dot(w[t], x1[t, row], preferred_element_type=F32)
            for i in range(3):
                acc[row + 2 - i] += total[i * 192 : (i + 1) * 192]

    def halo_low(w, frames):
        for t in frames:
            acc[0] += jnp.dot(w[t, 384:576], x1[t, 0], preferred_element_type=F32)
            acc[3] += jnp.dot(w[t, 0:192], x1[t, 1], preferred_element_type=F32)

    def inner_low(w, t):
        total = jnp.dot(w[t, 0:384], x1[t, 0], preferred_element_type=F32)
        acc[2] += total[0:192]
        acc[1] += total[192:384]
        total = jnp.dot(w[t, 192:576], x1[t, 1], preferred_element_type=F32)
        acc[2] += total[0:192]
        acc[1] += total[192:384]

    def halo_copies(slot, base):
        return [
            remote(hsend.at[0], hrecv.at[base + 1], slot, {"rows": up}),
            remote(hsend.at[1], hrecv.at[base], slot + 1, {"rows": dn}),
        ]

    has_up = (r > 0).astype(F32)
    has_dn = (r < 15).astype(F32)

    acc[...] = jnp.zeros_like(acc)
    local_lat.wait()
    for copy in local_gains:
        copy.wait()
    send_lat.wait_recv()
    for copy in send_gains:
        copy.wait_recv()
    gain = low_gain(gla, glao)

    @pl.loop(0, 2)
    def _(row):
        build_low(act(latf[row].astype(F32), gain), 2, row)

    low_a_here.wait()
    dots_low(w1a, 2)

    for d in range(3):
        remote(own12, own12, R_Z + d, z_targets[d]).wait_recv()
    for n in range(4):
        zc[16 * n : 16 * n + 12, :] = zb[n]
    rows48 = lax.broadcasted_iota(jnp.int32, (48, 64), 0)
    cols64 = lax.broadcasted_iota(jnp.int32, (48, 64), 1)
    pick = jnp.logical_and(rows48 == 12 * (cols64 // 16) + cols64 % 16, cols64 % 16 < 12)
    own48 = pl.ds(pl.multiple_of(x * 48, 16), 48)
    wh[piece, own48, :] = jnp.dot(
        jnp.where(pick, 1.0, 0.0).astype(BF), zc[...], preferred_element_type=F32
    ).astype(BF)

    def rows_of(xi):
        return pl.ds(pl.multiple_of(xi * 48, 16), 48)

    own4 = pl.ds(4 * k, 4)

    def same(ref, slot, target):
        return remote(ref, ref, slot, target)

    to_xn, to_xp, to_yn, to_yp = {"rows": xn}, {"rows": xp}, {"views": yn}, {"views": yp}
    w0 = [
        same(wh.at[piece, own48, 0:896], R_W0, to_xn),
        same(wh.at[piece, own48, 0:896], R_W0 + 1, to_xp),
        same(wh.at[piece, own48, 896:1792], R_W0 + 2, to_yn),
        same(wh.at[piece, own48, 896:1792], R_W0 + 3, to_yp),
    ]
    w1 = [
        same(wh.at[piece, rows_of(xpi), 0:512], R_W1, to_xn),
        same(wh.at[piece, rows_of(xni), 512:896], R_W1 + 1, to_xp),
        same(wh.at[4 * k + ypi, own48, 896:1408], R_W1 + 2, to_yn),
        same(wh.at[4 * k + yni, own48, 1408:1792], R_W1 + 3, to_yp),
    ]
    w2 = [
        same(wh.at[piece, :, 0:896], R_W2, to_yn),
        same(wh.at[piece, :, 0:896], R_W2 + 1, to_yp),
        same(wh.at[own4, own48, 896:1792], R_W2 + 2, to_xn),
        same(wh.at[own4, own48, 896:1792], R_W2 + 3, to_xp),
    ]
    w3 = [
        same(wh.at[4 * k + ypi, :, 0:512], R_W3, to_yn),
        same(wh.at[4 * k + yni, :, 512:896], R_W3 + 1, to_yp),
        same(wh.at[own4, rows_of(xpi), 896:1408], R_W3 + 2, to_xn),
        same(wh.at[own4, rows_of(xni), 1408:1792], R_W3 + 3, to_xp),
    ]
    w4 = [
        same(wh.at[own4, :, 0:896], R_W4, {"views": ov}),
        same(wh.at[own4, :, 896:1792], R_W4 + 1, {"views": ov}),
    ]

    def advance(done, begun):
        for copy in done:
            copy.wait_recv()
        for copy in begun:
            copy.start()

    advance([], w0)

    local_ha.wait()
    local_hb.wait()

    lane128 = lax.broadcasted_iota(jnp.int32, (1, 128), 1)
    edge_tile = pl.ds(pl.multiple_of((1 - c) * 128, 128), 128)

    def put_edge(pack, tile, m):
        return jnp.where(lane128 == m, pltpu.roll(tile, m + 1 - c, 1), pack)

    edges = jnp.zeros((192, 128), F32)
    for n, frames in enumerate((cha, chb)):
        for m in range(8):
            edges = put_edge(edges, frames[m // 4, m % 4, :, edge_tile].astype(F32), 8 * n + m)
    cpk[...] = edges.T[0:16]

    send_cpk = remote(cpk, cpkr.at[0:16], R_CPK, partner)
    send_cpk.start()

    advance(w0, w1)

    local_ca.wait()
    for t in range(2):
        send_ca[t].wait_recv()
    send_cb = [remote(cb_h.at[t], cbf.at[t, :, half, :], R_CB + t, partner) for t in range(2)]
    send_cb[0].start()
    @pl.loop(0, 4)
    def _(n):
        t, row = n // 2, lax.rem(n, 2)
        build_low(caf[t, row].astype(F32), t, row)

    halo_low(w1a, (0, 1))
    hsend[0] = acc[0].astype(BF)
    hsend[1] = acc[3].astype(BF)
    halo_a = halo_copies(R_HA, 0)
    for copy in halo_a:
        copy.start()
    for t in range(2):
        inner_low(w1a, t)
    for copy in halo_a:
        copy.wait_send()
    send_cb[1].start()
    advance(w1, w2)
    for copy in halo_a:
        copy.wait_recv()
    midf[0, half, :] = (acc[1] + has_up * hrecv[0].astype(F32)).astype(BF)
    midf[1, half, :] = (acc[2] + has_dn * hrecv[1].astype(F32)).astype(BF)
    send_mid = remote(midf.at[:, half, :], midf.at[:, half, :], R_MID, partner)
    send_mid.start()

    acc[...] = jnp.zeros_like(acc)
    local_cb.wait()
    for t in range(2):
        send_cb[t].wait_recv()

    @pl.loop(0, 4)
    def _(n):
        t, row = n // 2, lax.rem(n, 2)
        build_low(cbf[t, row].astype(F32), t, row)

    low_b_here.wait()
    for t in range(2):
        dots_low(w1b, t)

    send_mid.wait_recv()
    gain = low_gain(glb, glbo)

    @pl.loop(0, 2)
    def _(row):
        build_low(act(midf[row].astype(F32), gain), 2, row)

    halo_low(w1b, (2,))
    hsend[0] = acc[0].astype(BF)
    hsend[1] = acc[3].astype(BF)
    halo_b = halo_copies(R_HB, 2)
    for copy in halo_b:
        copy.start()
    inner_low(w1b, 2)
    advance(w2, w3)

    send_cpk.wait_recv()
    is0, is1 = (c == 0).astype(F32), (c == 1).astype(F32)
    columns[...] = cpkr[...].T

    def planes_high(values, margins, m):
        left = pltpu.roll(margins, lax.rem(128 - m, 128), 1) * is1
        right = pltpu.roll(margins, 127 - m, 1) * is0
        sides = jnp.concatenate([left, right], axis=1)
        j0, j2 = shifted(values, sides, sides)
        return j0, values.astype(BF), j2

    def build_high(values, margins, m, t, row):
        j0, j1, j2 = planes_high(values, margins, m)
        base = t * 576
        x2[row, pl.ds(base, 192), :] = j0
        x2[row, pl.ds(base + 192, 192), :] = j1
        x2[row, pl.ds(base + 384, 192), :] = j2

    def cached_high(frames, n):
        margins = columns[...]
        for t in range(2):
            @pl.loop(0, 4)
            def _(row, t=t):
                build_high(frames[t, row].astype(F32), margins, 8 * n + 4 * t + row, t, row)

    def cached_dots(first):
        @pl.loop(0, 4)
        def _(row):
            total = jnp.dot(
                wh[first : first + 3, :, 0:1152].reshape(576, 1152), x2[row, 0:1152, :],
                preferred_element_type=F32,
            )
            for i in range(3):
                acc2[row + 2 - i] += total[i * 192 : (i + 1) * 192]

    for row in range(4):
        x2[row, 1728:1792, :] = jnp.zeros((64, 256), BF)
    acc2[...] = jnp.zeros_like(acc2)
    cached_high(cha, 0)

    for copy in halo_b:
        copy.wait_recv()
    for n, (scale, row) in enumerate(((has_up, 1), (has_dn, 2))):
        lv[n] = (
            latf[n, half, :].astype(F32) + (acc[row] + scale * hrecv[2 + n].astype(F32))
        ).astype(BF)

    chalf = pl.ds(pl.multiple_of(c * 128, 128), 128)
    ohalf = pl.ds(pl.multiple_of(oc * 128, 128), 128)
    for n in range(2):
        values = lv[n].astype(F32)
        lpk[2 * n : 2 * n + 1, :] = to_row(values[:, 127:128])
        lpk[2 * n + 1 : 2 * n + 2, :] = to_row(values[:, 128:129])
    tiles = [
        remote(lv.at[:, :, ohalf], lt.at[pl.ds(1, 2), half, :], R_TILE, partner),
        remote(lv.at[0, :, chalf], lt.at[3, half, :], R_TILE + 1, {"rows": up}),
        remote(lv.at[1, :, chalf], lt.at[0, half, :], R_TILE + 2, {"rows": dn}),
        remote(lv.at[0, :, ohalf], lt.at[3, half, :], R_TILE + 3, {"rows": up, "chan": oc}),
        remote(lv.at[1, :, ohalf], lt.at[0, half, :], R_TILE + 4, {"rows": dn, "chan": oc}),
    ]
    packs = [
        remote(lpk, lpkr.at[n], R_PACK + n, around[n]) for n in range(5)
    ]
    for copy in packs + tiles:
        copy.start()
    lt[1, half, :] = lv[0, :, chalf]
    lt[2, half, :] = lv[1, :, chalf]
    advance(w3, w4)
    for copy in packs + tiles:
        copy.wait_recv()

    k128 = lax.broadcasted_iota(jnp.int32, (128, 256), 0)
    s256 = lax.broadcasted_iota(jnp.int32, (128, 256), 1)
    spread = [jnp.where(k128 == (s256 + j + 1) // 2 - 1, 1.0, 0.0).astype(BF) for j in range(3)]
    is_c0 = c == 0
    for slot in range(4):
        if slot in (1, 2):
            n = 2 * (slot - 1)
            mine, other = lpk[n : n + 2, :], lpkr[0, n : n + 2, :]
        elif slot == 0:
            mine, other = lpkr[2, 2:4, :], lpkr[4, 2:4, :]
        else:
            mine, other = lpkr[1, 0:2, :], lpkr[3, 0:2, :]
        mine = to_column(jnp.where(is_c0, mine[1:2], mine[0:1]))
        other = to_column(jnp.where(is_c0, other[1:2], other[0:1]))
        margin = jnp.concatenate(
            [jnp.where(is_c0, mine, other), jnp.where(is_c0, other, mine)], axis=0
        )
        scale = has_up if slot == 0 else has_dn if slot == 3 else 1.0
        margin = margin * scale
        tile = lt[slot]
        for j in range(3):
            wide = jnp.dot(tile, spread[j], preferred_element_type=F32) * scale
            if j == 0:
                wide = jnp.where(lane == 0, margin * is1, wide)
            if j == 2:
                wide = jnp.where(lane == 255, margin * is0, wide)
            xl[slot, j * 384 : (j + 1) * 384, :] = wide.astype(BF)

    for copy in w4:
        copy.wait_recv()

    gain2 = column_of(gha)

    for slot in range(4):
        for i in range(3):
            rows_out = [u for u in range(4) if (u + i + 1) // 2 == slot]
            if not rows_out:
                continue
            if i == 0:
                total = jnp.dot(wh[0, :, 0:1152], xl[slot], preferred_element_type=F32)
            elif i == 1:
                total = jnp.dot(wh[0, :, 1152:1792], xl[slot, 0:640, :], preferred_element_type=F32)
                total += jnp.dot(wh[1, :, 0:512], xl[slot, 640:1152, :], preferred_element_type=F32)
            else:
                total = jnp.dot(wh[1, :, 512:1664], xl[slot], preferred_element_type=F32)
            for u in rows_out:
                if slot == (u + 1) // 2 and i == 0:
                    outv[u] = total
                else:
                    outv[u] += total

    def living_high(value_of, gain, pack_slot, n, rows):
        @pl.loop(0, rows)
        def _(row):
            values = act(value_of(row), gain)
            outv[row] = values

        edges = jnp.zeros((192, 128), F32)
        for row in range(rows):
            edges = put_edge(edges, outv[row, :, edge_tile], row)
        pk[n] = edges.T[0:8]
        send = remote(pk.at[n], pkr.at[n, 0:8], pack_slot, partner)
        send.start()
        return send

    def finish_living(send, n):
        send.wait_recv()

        margins = pkr[n].T

        @pl.loop(0, 4)
        def _(row):
            build_high(outv[row], margins, row, 2, row)

    def round_resampled(row):
        values = outv[row].astype(BF)
        rsd[row] = values
        return values.astype(F32)

    send_a = living_high(round_resampled, gain2, R_PKA, 0, 4)
    cached_dots(2)
    finish_living(send_a, 0)
    def sums_high(first, todo, living):
        for row, i, out in todo:
            acc2[out] += jnp.dot(
                wh[first + i, :, 1152:1792], living(row), preferred_element_type=F32
            )

    pairs = [(row, i, row + 2 - i) for row in range(4) for i in range(3)]
    sums_high(2, [p for p in pairs if p[2] in (0, 1, 4, 5)], lambda row: x2[row, 1152:1792, :])
    for n, row in enumerate((0, 1, 4, 5)):
        esend[n] = acc2[row].astype(BF)
    halo_2a = [
        remote(esend.at[0:2], erecv.at[2:4], R_H2A, {"rows": up}),
        remote(esend.at[2:4], erecv.at[0:2], R_H2A + 1, {"rows": dn}),
    ]
    for copy in halo_2a:
        copy.start()
    sums_high(2, [p for p in pairs if p[2] in (2, 3)], lambda row: x2[row, 1152:1792, :])
    for row in range(6):
        outv[row] = acc2[row]

    acc2[...] = jnp.zeros_like(acc2)
    cached_high(chb, 1)
    cached_dots(5)
    for copy in halo_2a:
        copy.wait_recv()
    for copy in halo_b:
        copy.wait_send()
    hsend[0] = acc2[0].astype(BF)
    hsend[1] = acc2[5].astype(BF)
    halo_2b = halo_copies(R_H2B, 6)
    outv[0] = has_up * (outv[0] + erecv[0].astype(F32))
    outv[1] += has_up * erecv[1].astype(F32)
    outv[4] += has_dn * erecv[2].astype(F32)
    outv[5] = has_dn * (outv[5] + erecv[3].astype(F32))

    gain2 = column_of(ghb)
    send_b = living_high(lambda row: outv[row].astype(BF).astype(F32), gain2, R_PKB, 1, 6)
    for copy in halo_2b:
        copy.start()
    for row in range(6):
        x2l[row, 576:640, :] = jnp.zeros((64, 256), BF)
    send_b.wait_recv()
    margins = pkr[1].T

    @pl.loop(0, 6)
    def _(row):
        j0, j1, j2 = planes_high(outv[row], margins, row)
        x2l[row, 0:192, :] = j0
        x2l[row, 192:384, :] = j1
        x2l[row, 384:576, :] = j2

    @pl.loop(0, 4)
    def _(row):
        total = jnp.dot(wh[5, :, 1152:1792], x2l[row], preferred_element_type=F32)
        for i in range(1, 3):
            total += jnp.dot(wh[5 + i, :, 1152:1792], x2l[row + i], preferred_element_type=F32)
        acc2[row + 1] += total

    for row in range(1, 3):
        rsd[row] = (rsd[row].astype(F32) + acc2[row + 1]).astype(BF)
    for copy in halo_2b:
        copy.wait_recv()
    rsd[0] = (rsd[0].astype(F32) + (acc2[1] + has_up * hrecv[6].astype(F32))).astype(BF)
    rsd[3] = (rsd[3].astype(F32) + (acc2[4] + has_dn * hrecv[7].astype(F32))).astype(BF)
    write = local(rsd, out_h, L_OUT)
    write.start()

    sends = (
        [send_lat, send_cpk, send_mid, send_a, send_b]
        + send_gains + send_ca + send_cb + z_copies + w0 + w1 + w2 + w3 + w4 + tiles + packs + halo_2a + halo_2b
    )
    for copy in sends:
        copy.wait_send()
    write.wait()


def body(
    latent, cache_low_a, cache_low_b, gain_low_a, gain_low_b, kernel_low_a, kernel_low_b,
    resample_kernel, gain_high_a, gain_high_b, kernel_high_a, kernel_high_b,
    cache_high_a, cache_high_b,
):
    vm = pltpu.VMEM
    return pl.pallas_call(
        kernel,
        out_shape=jax.ShapeDtypeStruct((4, 192, 256), BF),
        in_specs=[pl.BlockSpec(memory_space=pl.ANY)] * 14,
        out_specs=pl.BlockSpec(memory_space=pl.ANY),
        scratch_shapes=[
            vm((2, 384, 256), BF),
            vm((2, 2, 384, 256), BF),
            vm((2, 2, 384, 256), BF),
            vm((192,), BF),
            vm((192,), BF),
            vm((192,), BF),
            vm((192,), BF),
            vm((192,), BF),
            vm((192,), BF),
            vm((3, 576, 1152), BF),
            vm((3, 576, 1152), BF),
            vm((3, 2, 1152, 256), BF),
            vm((4, 192, 256), F32),
            vm((2, 192, 256), BF),
            vm((8, 192, 256), BF),
            vm((2, 384, 256), BF),
            vm((3, 3, 12, 192), BF),
            vm((3, 3, 12, 384), BF),
            vm((16, 1792), F32),
            vm((4, 12, 1792), BF),
            vm((64, 1792), BF),
            vm((8, 192, 1792), BF),
            vm((2, 4, 192, 256), BF),
            vm((2, 4, 192, 256), BF),
            vm((4, 1792, 256), BF),
            vm((6, 192, 256), F32),
            vm((2, 192, 256), BF),
            vm((4, 384, 128), BF),
            vm((8, 192), F32),
            vm((5, 8, 192), F32),
            vm((4, 1152, 256), BF),
            vm((4, 192, 256), BF),
            vm((16, 192), F32),
            vm((128, 192), F32),
            vm((192, 128), F32),
            vm((2, 8, 192), F32),
            vm((2, 128, 192), F32),
            vm((6, 192, 256), F32),
            vm((6, 640, 256), BF),
            vm((4, 192, 256), BF),
            vm((4, 192, 256), BF),
            pltpu.SemaphoreType.DMA((N_REMOTE,)),
            pltpu.SemaphoreType.DMA((N_REMOTE,)),
            pltpu.SemaphoreType.DMA((N_LOCAL,)),
            pltpu.SemaphoreType.REGULAR((3,)),
        ],
        compiler_params=pltpu.CompilerParams(
            collective_id=0, has_side_effects=True, vmem_limit_bytes=58 * 1024 * 1024
        ),
    )(
        latent, cache_low_a, cache_low_b, gain_low_a, gain_low_b, kernel_low_a, kernel_low_b,
        resample_kernel, gain_high_a, gain_high_b, kernel_high_a, kernel_high_b, cache_high_a, cache_high_b,
    )


def solution(mesh):
    placed = (
        P(("views", "rows"), "chan", None),
        P(None, ("views", "rows"), "chan", None),
        P(None, ("views", "rows"), "chan", None),
        P("chan"),
        P("chan"),
        P(None, None, None, "chan", None),
        P(None, None, None, "chan", None),
        P(None, None, "rows", None),
        P(),
        P(),
        P(None, None, None, "rows", None),
        P(None, None, None, "rows", None),
        P(None, ("views", "rows"), None, "chan"),
        P(None, ("views", "rows"), None, "chan"),
    )
    return jax.shard_map(
        body,
        mesh=mesh,
        in_specs=placed,
        out_specs=P(("views", "rows"), None, "chan"),
        check_vma=False,
    )
```
